32 devices in a mesh: row: 4 (over z), col: 8 (over y, x, core).
Axes of the slice: x: 2, y: 2, z: 4, core: 2. Of those that a mesh axis runs over, the one named last changes fastest.
Arguments:
- matrix: float32 [6144, 6144], P('row', 'col'), may hold values from -160 to 160, as said below
- pattern: int32 [16, 16], replicated, may hold values from 0 to 1, as said below
- row_order: int32 [16], replicated, may hold values from 0 to 15, as said below
- col_order: int32 [16], replicated, may hold values from 0 to 15, as said below
Outputs:
- factored: float32 [6144, 6144], P('row', 'col')
The draws below stay inside these ranges and needn't reach their ends.
Inputs may be any that keep to these rules, and one draw needn't show every extreme that they name: `row_order`: a permutation of 0 to 15. `col_order`: a permutation of 0 to 15. Symmetric with ones on the diagonal; pattern[1, 0] = 1; pattern[I, J] = 1 whenever pattern[I, 0] = pattern[J, 0] = 1, and whenever pattern[I, 1] = pattern[J, 1] = 1 with I, J >= 1. `matrix`: read in natural block order the window is symmetric, and its retained lower blocks make the pivot block of supernode 0, and that of supernode 1 after the first update, positive definite.
All inputs are finite; a program needn't handle non-finite values.
Results may differ from the reference program's by a relative error of at most 0.0003.
Values sent between devices are 32-bit elements; how exact they have to be, the bound alone decides.
No kernel may reach another device: no remote copies, remote signals or barrier semaphores. Data moves between devices by JAX's collectives and lax.ppermute only.
A program may use at most 128 MiB of HBM per device.

```python
import math
import jax
import jax.numpy as jnp
from jax import lax

BLOCK = 384
WINDOW = 16


def layout(key):
    indices = jnp.arange(WINDOW, dtype=jnp.int32)
    row_order = jax.random.permutation(jax.random.fold_in(key, 11), WINDOW).astype(jnp.int32)
    col_order = jax.random.permutation(jax.random.fold_in(key, 12), WINDOW).astype(jnp.int32)
    first = jax.random.randint(jax.random.fold_in(key, 13), (WINDOW,), 0, 2).astype(jnp.int32)
    first = jnp.where(indices <= 1, 1, first)
    second = jnp.maximum(first, jax.random.randint(jax.random.fold_in(key, 14), (WINDOW,), 0, 2).astype(jnp.int32))
    second = jnp.where(indices == 0, 0, jnp.where(indices == 1, 1, second))
    extra = jax.random.randint(jax.random.fold_in(key, 15), (WINDOW, WINDOW), 0, 4) == 0
    trailing = (indices[:, None] >= 2) & (indices[None, :] >= 2) & (indices[:, None] > indices[None, :])
    extra = extra & trailing
    extra = extra | extra.T
    linked = first[:, None] * first[None, :] + second[:, None] * second[None, :] > 0
    pattern = (linked | extra | (indices[:, None] == indices[None, :])).astype(jnp.int32)
    return (row_order, col_order, pattern, first, second)


def pivot_factor(key):
    lower_part = jnp.tril(jnp.ones((BLOCK, BLOCK), jnp.float32), -1)
    diagonal = jax.random.uniform(jax.random.fold_in(key, 1), (BLOCK,), jnp.float32, 1.0, 2.0)
    spread = jax.random.truncated_normal(jax.random.fold_in(key, 2), -4.0, 4.0, (BLOCK, BLOCK), jnp.float32)
    return jnp.diag(diagonal) + spread * (0.5 / math.sqrt(BLOCK)) * lower_part


def draw_matrix(key, part):
    row_order, col_order, pattern, first, second = layout(key)
    indices = jnp.arange(WINDOW, dtype=jnp.int32)
    order = WINDOW * BLOCK
    first_rows = jnp.repeat(((first == 1) & (indices >= 1)).astype(jnp.float32), BLOCK)
    second_rows = jnp.repeat(((second == 1) & (indices >= 2)).astype(jnp.float32), BLOCK)
    first_factor = jax.random.truncated_normal(jax.random.fold_in(key, 21), -4.0, 4.0, (order, BLOCK), jnp.float32) * 0.25 * first_rows[:, None]
    first_factor = first_factor.at[0:BLOCK].set(pivot_factor(jax.random.fold_in(key, 22)))
    second_factor = jax.random.truncated_normal(jax.random.fold_in(key, 23), -4.0, 4.0, (order, BLOCK), jnp.float32) * 0.25 * second_rows[:, None]
    second_factor = second_factor.at[BLOCK:2 * BLOCK].set(pivot_factor(jax.random.fold_in(key, 24)))
    noise = jax.random.truncated_normal(jax.random.fold_in(key, 25), -4.0, 4.0, (order, order), jnp.float32)
    noise = (noise + noise.T) * 0.7071
    relevant = ((indices[:, None] <= 1) | (indices[None, :] <= 1)) & (pattern == 1)
    keep_noise = 1.0 - jnp.repeat(jnp.repeat(relevant.astype(jnp.float32), BLOCK, axis=0), BLOCK, axis=1)
    natural = jnp.dot(first_factor, first_factor.T, precision=lax.Precision.HIGHEST)
    natural = natural + jnp.dot(second_factor, second_factor.T, precision=lax.Precision.HIGHEST)
    natural = natural + noise * keep_noise
    tiles = natural.reshape(WINDOW, BLOCK, WINDOW, BLOCK)
    stored = jnp.take(jnp.take(tiles, row_order, axis=0), col_order, axis=2)
    return stored.reshape(order, order)


def draw_pattern(key, part):
    return layout(key)[2]


def draw_row_order(key, part):
    return layout(key)[0]


def draw_col_order(key, part):
    return layout(key)[1]


def setup_inputs(seed: int = 0) -> dict:
    seeds = jax.random.split(jax.random.key(seed), 5)
    matrix = draw_matrix(jax.random.fold_in(seeds[4], 71), 0)
    pattern = draw_pattern(jax.random.fold_in(seeds[4], 71), 0)
    row_order = draw_row_order(jax.random.fold_in(seeds[4], 71), 0)
    col_order = draw_col_order(jax.random.fold_in(seeds[4], 71), 0)
    return {"matrix": matrix, "pattern": pattern, "row_order": row_order, "col_order": col_order}


def positions(order):
    indices = jnp.arange(order.shape[0], dtype=jnp.int32)
    return jnp.sum(jnp.where(order[None, :] == indices[:, None], indices[None, :], 0), axis=1).astype(jnp.int32)

def expand(flags, tall, broad):
    return jnp.repeat(jnp.repeat(flags, tall, axis=0), broad, axis=1)

def reference(matrix, pattern, row_order, col_order):
    total = row_order.shape[0]
    row_place = positions(row_order)
    col_place = positions(col_order)
    tiles = matrix.reshape(total, BLOCK, total, BLOCK)
    natural = jnp.take(jnp.take(tiles, row_place, axis=0), col_place, axis=2)
    natural = natural.reshape(total * BLOCK, total * BLOCK)
    indices = jnp.arange(total, dtype=jnp.int32)
    lower = indices[:, None] >= indices[None, :]
    retain = expand((pattern == 1) & lower, BLOCK, BLOCK).astype(natural.dtype)
    lower_full = expand(lower, BLOCK, BLOCK).astype(natural.dtype)
    current = natural * retain
    identity = jnp.eye(BLOCK, dtype=natural.dtype)
    for supernode in range(2):
        low_edge = supernode * BLOCK
        pivot_values = current[low_edge:low_edge + BLOCK, low_edge:low_edge + BLOCK]
        factor = jnp.linalg.cholesky(pivot_values)
        inverse = jax.scipy.linalg.solve_triangular(factor, identity, lower=True)
        struct_rows = ((pattern[:, supernode] == 1) & (indices > supernode)).astype(natural.dtype)
        panel = current[:, low_edge:low_edge + BLOCK] * jnp.repeat(struct_rows, BLOCK)[:, None]
        scaled = jnp.dot(panel, inverse.T, precision=lax.Precision.HIGHEST)
        current = current - jnp.dot(scaled, scaled.T, precision=lax.Precision.HIGHEST) * lower_full
        center = jnp.repeat(indices == supernode, BLOCK)
        column = jnp.where(center[:, None], jnp.tile(factor, (total, 1)), scaled)
        current = current.at[:, low_edge:low_edge + BLOCK].set(column)
    current = current * retain
    tiles = current.reshape(total, BLOCK, total, BLOCK)
    stored = jnp.take(jnp.take(tiles, row_order, axis=0), col_order, axis=2)
    return stored.reshape(total * BLOCK, total * BLOCK)
```

```python
import jax
import jax.numpy as jnp
from jax import lax
from jax.experimental import pallas as pl
from jax.experimental.pallas import tpu as pltpu
from jax.sharding import PartitionSpec as P

LANES = 128
CHUNKS = 4


def dot_nt(a, b, precision):
    dims = (((1,), (1,)), ((), ()))
    return lax.dot_general(a, b, dims, precision=precision, preferred_element_type=jnp.float32)


def dot_nn(a, b, precision):
    dims = (((1,), (0,)), ((), ()))
    return lax.dot_general(a, b, dims, precision=precision, preferred_element_type=jnp.float32)


def unit(size):
    rows = lax.broadcasted_iota(jnp.int32, (size, size), 0)
    lanes = lax.broadcasted_iota(jnp.int32, (size, size), 1)
    return (rows == lanes).astype(jnp.float32)


def invert_diagonal(schur, carried, inverse):
    tile = (8, LANES)
    sublane = lax.broadcasted_iota(jnp.int32, tile, 0)
    carried[...] = unit(LANES)

    def row_of(x, p):
        return jnp.broadcast_to(x[p : p + 1, :], tile)

    def lane_of(x, p):
        return jnp.broadcast_to(x[:, p : p + 1], tile)

    steps = LANES // 8
    for b in range(steps):
        rows = schur[8 * b : 8 * b + 8, :]
        extra = carried[8 * b : 8 * b + 8, :]
        columns = [lane_of(rows, 8 * b + p) for p in range(8)]
        reciprocals = jnp.zeros(tile, jnp.float32)
        pivots = jnp.ones(tile, jnp.float32)
        for p in range(8):
            pivot = row_of(columns[p], p)
            reciprocal = 1.0 / pivot
            factor = jnp.where(sublane > p, columns[p] * reciprocal, 0.0)
            for q in range(p + 1, 8):
                columns[q] = columns[q] - factor * row_of(columns[q], p)
            rows = rows - factor * row_of(rows, p)
            extra = extra - factor * row_of(extra, p)
            reciprocals = jnp.where(sublane == p, reciprocal, reciprocals)
            pivots = jnp.where(sublane == p, pivot, pivots)
        inverse[8 * b : 8 * b + 8, :] = extra * lax.rsqrt(pivots)
        if b == steps - 1:
            break
        solved = rows * reciprocals
        solved_extra = extra * reciprocals
        for p in range(7, 0, -1):
            factor = jnp.where(sublane < p, columns[p] * reciprocals, 0.0)
            solved = solved - factor * row_of(solved, p)
            solved_extra = solved_extra - factor * row_of(solved_extra, p)
        right = [row_of(solved, p) for p in range(8)]
        right_extra = [row_of(solved_extra, p) for p in range(8)]
        for i in range(b + 1, steps):
            part = schur[8 * i : 8 * i + 8, :]
            part_extra = carried[8 * i : 8 * i + 8, :]
            left = [lane_of(part, 8 * b + p) for p in range(8)]
            for p in range(8):
                part = part - left[p] * right[p]
                part_extra = part_extra - left[p] * right_extra[p]
            schur[8 * i : 8 * i + 8, :] = part
            carried[8 * i : 8 * i + 8, :] = part_extra


def factor_block(work, out, schur, carried, inverse):
    size = work.shape[0]
    out[...] = unit(size)
    steps = size // LANES
    full = lax.Precision.HIGHEST

    def step(k, carry):
        low = pl.multiple_of(k * LANES, LANES)
        schur[...] = work[pl.ds(low, LANES), pl.ds(low, LANES)]
        invert_diagonal(schur, carried, inverse)
        out[pl.ds(low, LANES), :] = dot_nn(inverse[...], out[pl.ds(low, LANES), :], full)
        for done in range(steps - 1):

            @pl.when(k == done)
            def _():
                top, edge = done * LANES, (done + 1) * LANES
                panel = dot_nt(work[edge:, top:edge], inverse[...], full)
                work[edge:, edge:] = work[edge:, edge:] - dot_nt(panel, panel, full)
                out[edge:, :edge] = out[edge:, :edge] - dot_nn(panel, out[top:edge, :edge], full)

        return carry

    lax.fori_loop(0, steps, step, 0)


def first_kernel(pivot, inverse_out, work, schur, carried, inverse):
    work[...] = pivot[...]
    factor_block(work, inverse_out, schur, carried, inverse)


def second_kernel(below, pivot, inverse_first, lower_out, inverse_out, work, schur, carried, inverse):
    full = lax.Precision.HIGHEST
    lower_out[...] = dot_nt(below[...], inverse_first[...], full)
    work[...] = pivot[...] - dot_nt(lower_out[...], lower_out[...], full)
    factor_block(work, inverse_out, schur, carried, inverse)


def scratch(size):
    small = pltpu.VMEM((LANES, LANES), jnp.float32)
    return [pltpu.VMEM((size, size), jnp.float32), small, small, small]


def first_inverse(pivot):
    size = pivot.shape[0]
    square = jax.ShapeDtypeStruct((size, size), jnp.float32)
    return pl.pallas_call(first_kernel, out_shape=square, scratch_shapes=scratch(size), name="first")(pivot)


def second_inverse(below, pivot, inverse_first):
    size = pivot.shape[0]
    square = jax.ShapeDtypeStruct((size, size), jnp.float32)
    return pl.pallas_call(
        second_kernel, out_shape=(square, square), scratch_shapes=scratch(size), name="second"
    )(below, pivot, inverse_first)


def swap(value, axis, count, bit):
    return lax.ppermute(value, axis, [(i, i ^ bit) for i in range(count)])


def bits_of(count):
    return [1 << b for b in range(count.bit_length() - 1)]


class Grid:
    def __init__(self, rows, cols):
        self.rows, self.cols = rows, cols
        self.row = lax.axis_index("row")
        self.col = lax.axis_index("col")

    def along_row_axis(self, value, root):
        for bit in bits_of(self.rows):
            received = swap(value, "row", self.rows, bit)
            value = jnp.where(((root ^ self.row) & bit) != 0, received, value)
        return value

    def along_col_axis(self, value, root, bits):
        for bit in bits:
            received = swap(value, "col", self.cols, bit)
            value = jnp.where(((root ^ self.col) & bit) != 0, received, value)
        return value

    def spread(self, value, root_row, root_col):
        half = value.shape[0] // 2
        side = self.col & 1
        mine = lax.dynamic_slice_in_dim(value, side * half, half, 0)
        other = lax.dynamic_slice_in_dim(value, (1 - side) * half, half, 0)
        received = swap(other, "col", self.cols, 1)
        mine = jnp.where(((root_col ^ self.col) & 1) != 0, received, mine)
        if root_row is not None:
            mine = self.along_row_axis(mine, root_row)
        bits = bits_of(self.cols)[1:]
        quarter = half // 2
        one = self.along_col_axis(mine[:quarter], root_col, bits)
        two = self.along_col_axis(mine[quarter:], root_col, bits[::-1])
        mine = jnp.concatenate([one, two], axis=0)
        received = swap(mine, "col", self.cols, 1)
        low = jnp.where(side == 0, mine, received)
        high = jnp.where(side == 0, received, mine)
        return jnp.concatenate([low, high], axis=0)

    def pipeline(self, value, root):
        count = self.rows
        size = value.shape[0] // CHUNKS
        own = [value[i * size : (i + 1) * size] for i in range(CHUNKS)]
        right = [(i, i + 1) for i in range(count - 1)]
        left = [(i + 1, i) for i in range(count - 1)]
        distance = jnp.abs(self.row - root)
        arrived = []
        payload = own[0]
        for step in range(CHUNKS + count - 2):
            from_left = lax.ppermute(payload, "row", right)
            from_right = lax.ppermute(payload, "row", left)
            arrived.append(jnp.where(self.row > root, from_left, from_right))
            payload = jnp.where(distance == 0, own[min(step + 1, CHUNKS - 1)], arrived[-1])
        chunks = []
        for i in range(CHUNKS):
            chunk = own[i]
            for d in range(1, count):
                chunk = jnp.where(distance == d, arrived[i + d - 1], chunk)
            chunks.append(chunk)
        return jnp.concatenate(chunks, axis=0)


def make_body(rows, cols):
    def body(matrix, pattern, row_order, col_order):
        grid = Grid(rows, cols)
        local_rows, width = matrix.shape
        total = row_order.shape[0]
        block = local_rows * rows // total
        tall, broad = local_rows // block, width // block
        indices = jnp.arange(total, dtype=jnp.int32)
        orders = jnp.stack([row_order, col_order])
        places = jnp.sum(
            jnp.where(orders[:, None, :] == jnp.arange(2, dtype=jnp.int32)[None, :, None], indices, 0), axis=2
        )
        root_row = [places[0, s] // tall for s in range(2)]
        root_col = [places[1, s] // broad for s in range(2)]
        top = [places[0, s] % tall * block for s in range(2)]
        side = [places[1, s] % broad * block for s in range(2)]
        pivot = {}
        for r, c in ((0, 0), (1, 0), (1, 1)):
            piece = lax.dynamic_slice(matrix, (top[r], side[c]), (block, block))
            pivot[r, c] = grid.spread(piece, root_row[r], root_col[c])
        panels = []
        slabs = []
        for s in range(2):
            slab = lax.dynamic_slice_in_dim(matrix, top[s], block, 0)
            slabs.append(grid.pipeline(slab, root_row[s]))
            panel = lax.dynamic_slice_in_dim(matrix, side[s], block, 1)
            panels.append(grid.spread(panel, None, root_col[s]))

        inverse0 = first_inverse(pivot[0, 0])
        lower, inverse1 = second_inverse(pivot[1, 0], pivot[1, 1], inverse0)

        row_ids = lax.dynamic_slice_in_dim(row_order, grid.row * tall, tall, 0)
        col_ids = lax.dynamic_slice_in_dim(col_order, grid.col * broad, broad, 0)
        row_marks = (row_ids[:, None] == indices[None, :]).astype(jnp.int32)
        col_marks = (col_ids[:, None] == indices[None, :]).astype(jnp.int32)
        marked = jnp.dot(jnp.dot(row_marks, pattern), col_marks.T)
        row_linked = jnp.dot(row_marks, pattern[:, :2])
        col_linked = jnp.dot(col_marks, pattern[:, :2])
        retain = (marked == 1) & (row_ids[:, None] >= col_ids[None, :])

        def long(flags):
            return jnp.repeat(flags, block)

        used = [long((row_linked[:, s] == 1) & (row_ids > s)) for s in range(2)]
        used_cols = [long((col_linked[:, s] == 1) & (col_ids > s)) for s in range(2)]
        mid = lax.Precision.HIGH
        full0 = dot_nt(panels[0], inverse0, mid)
        scaled0 = jnp.where(used[0][:, None], full0, 0.0)
        across0 = jnp.where(used_cols[0][None, :], dot_nn(inverse0, slabs[0], mid), 0.0)
        column1 = panels[1] - dot_nt(scaled0, lower, mid)
        cross1 = slabs[1] - dot_nn(lower, across0, mid)
        full1 = dot_nt(column1, inverse1, mid)
        scaled1 = jnp.where(used[1][:, None], full1, 0.0)
        across1 = jnp.where(used_cols[1][None, :], dot_nn(inverse1, cross1, mid), 0.0)
        left = jnp.concatenate([scaled0, scaled1], axis=1)
        right = jnp.concatenate([across0, across1], axis=0)
        result = matrix - dot_nn(left, right, mid)
        triangle = jnp.tile(lax.iota(jnp.int32, local_rows)[:, None] % block >= lax.iota(jnp.int32, block)[None, :], (1, 1))
        pieces = []
        for j in range(broad):
            present = result[:, j * block : (j + 1) * block]
            for s, full in ((0, full0), (1, full1)):
                center = long(row_ids == s)
                kept = jnp.where(center[:, None] & ~triangle, 0.0, full)
                present = jnp.where(col_ids[j] == s, kept, present)
            pieces.append(jnp.where(long(retain[:, j])[:, None], present, 0.0))
        return jnp.concatenate(pieces, axis=1)

    return body


def solution(mesh):
    in_specs = (P("row", "col"), P(), P(), P())
    out_specs = P("row", "col")
    body = make_body(mesh.shape["row"], mesh.shape["col"])
    return jax.shard_map(body, mesh=mesh, in_specs=in_specs, out_specs=out_specs, check_vma=False)
```

```python
import jax
import jax.numpy as jnp
from jax import lax
from jax.experimental import pallas as pl
from jax.experimental.pallas import tpu as pltpu
from jax.sharding import PartitionSpec as P

LANES = 128
CHUNKS = 3


def dot_nt(a, b, precision):
    dims = (((1,), (1,)), ((), ()))
    return lax.dot_general(a, b, dims, precision=precision, preferred_element_type=jnp.float32)


def dot_nn(a, b, precision):
    dims = (((1,), (0,)), ((), ()))
    return lax.dot_general(a, b, dims, precision=precision, preferred_element_type=jnp.float32)


def unit(size):
    rows = lax.broadcasted_iota(jnp.int32, (size, size), 0)
    lanes = lax.broadcasted_iota(jnp.int32, (size, size), 1)
    return (rows == lanes).astype(jnp.float32)


def invert_diagonal(schur, carried, inverse):
    tile = (8, LANES)
    sublane = lax.broadcasted_iota(jnp.int32, tile, 0)
    carried[...] = unit(LANES)

    def row_of(x, p):
        return jnp.broadcast_to(x[p : p + 1, :], tile)

    def lane_of(x, p):
        return jnp.broadcast_to(x[:, p : p + 1], tile)

    steps = LANES // 8
    for b in range(steps):
        rows = schur[8 * b : 8 * b + 8, :]
        extra = carried[8 * b : 8 * b + 8, :]
        columns = [lane_of(rows, 8 * b + p) for p in range(8)]
        reciprocals = jnp.zeros(tile, jnp.float32)
        pivots = jnp.ones(tile, jnp.float32)
        for p in range(8):
            pivot = row_of(columns[p], p)
            reciprocal = 1.0 / pivot
            factor = jnp.where(sublane > p, columns[p] * reciprocal, 0.0)
            for q in range(p + 1, 8):
                columns[q] = columns[q] - factor * row_of(columns[q], p)
            rows = rows - factor * row_of(rows, p)
            extra = extra - factor * row_of(extra, p)
            reciprocals = jnp.where(sublane == p, reciprocal, reciprocals)
            pivots = jnp.where(sublane == p, pivot, pivots)
        inverse[8 * b : 8 * b + 8, :] = extra * lax.rsqrt(pivots)
        if b == steps - 1:
            break
        solved = rows * reciprocals
        solved_extra = extra * reciprocals
        for p in range(7, 0, -1):
            factor = jnp.where(sublane < p, columns[p] * reciprocals, 0.0)
            solved = solved - factor * row_of(solved, p)
            solved_extra = solved_extra - factor * row_of(solved_extra, p)
        right = [row_of(solved, p) for p in range(8)]
        right_extra = [row_of(solved_extra, p) for p in range(8)]
        for i in range(b + 1, steps):
            part = schur[8 * i : 8 * i + 8, :]
            part_extra = carried[8 * i : 8 * i + 8, :]
            left = [lane_of(part, 8 * b + p) for p in range(8)]
            for p in range(8):
                part = part - left[p] * right[p]
                part_extra = part_extra - left[p] * right_extra[p]
            schur[8 * i : 8 * i + 8, :] = part
            carried[8 * i : 8 * i + 8, :] = part_extra


def factor_block(work, out, schur, carried, inverse):
    size = work.shape[0]
    out[...] = unit(size)
    steps = size // LANES
    full = lax.Precision.HIGHEST

    def step(k, carry):
        low = pl.multiple_of(k * LANES, LANES)
        schur[...] = work[pl.ds(low, LANES), pl.ds(low, LANES)]
        invert_diagonal(schur, carried, inverse)
        out[pl.ds(low, LANES), :] = dot_nn(inverse[...], out[pl.ds(low, LANES), :], full)
        for done in range(steps - 1):

            @pl.when(k == done)
            def _():
                top, edge = done * LANES, (done + 1) * LANES
                panel = dot_nt(work[edge:, top:edge], inverse[...], full)
                work[edge:, edge:] = work[edge:, edge:] - dot_nt(panel, panel, full)
                out[edge:, :edge] = out[edge:, :edge] - dot_nn(panel, out[top:edge, :edge], full)

        return carry

    lax.fori_loop(0, steps, step, 0)


def strips(block):
    tiles = block // LANES
    found, low = [], 0
    for part in range(3):
        for lane in range(tiles):
            first = 0 if part == 1 else lane * LANES
            found.append([part, first, lane * LANES, block - first, low])
            low += block - first
    half = low // 2
    split = []
    for part, first, lane, rows, at in found:
        cut = half - at
        if 0 < cut < rows:
            split.append((part, first, lane, cut, at))
            split.append((part, first + cut, lane, rows - cut, half))
        else:
            split.append((part, first, lane, rows, at))
    return split, low


def pack_kernel(places, matrix, keep, send, sems, *, block, pieces, half):
    for side in range(2):

        @pl.when(places[PLACE_SIDE] == side)
        def _():
            for n, (part, first, lane, rows, at) in enumerate(pieces):
                row = pl.multiple_of(places[TOP + min(part, 1)] + first, 8)
                column = pl.multiple_of(places[EDGE + part // 2] + lane, LANES)
                target = keep if at // half == side else send
                source = matrix.at[pl.ds(row, rows), pl.ds(column, LANES)]
                pltpu.make_async_copy(source, target.at[pl.ds(at % half, rows), :], sems.at[n]).start()
            for n, (part, first, lane, rows, at) in enumerate(pieces):
                target = keep if at // half == side else send
                source = matrix.at[pl.ds(0, rows), pl.ds(0, LANES)]
                pltpu.make_async_copy(source, target.at[pl.ds(at % half, rows), :], sems.at[n]).wait()


def pack(places, matrix, block):
    pieces, total = strips(block)
    half = total // 2
    out = jax.ShapeDtypeStruct((half, LANES), jnp.float32)
    return pl.pallas_call(
        lambda *refs: pack_kernel(*refs, block=block, pieces=pieces, half=half),
        out_shape=(out, out),
        in_specs=[pl.BlockSpec(memory_space=pltpu.SMEM), pl.BlockSpec(memory_space=pl.ANY)],
        scratch_shapes=[pltpu.SemaphoreType.DMA((len(pieces),))],
        name="pack",
    )(places, matrix)


def unpack(places, mine, other, message, pieces, half, wanted, work):
    side = places[PLACE_SIDE]
    message[pl.ds(pl.multiple_of(side * half, 8), half), :] = mine[...]
    message[pl.ds(pl.multiple_of((1 - side) * half, 8), half), :] = other[...]
    for part, first, lane, rows, at in pieces:
        if part == wanted:
            work[first : first + rows, lane : lane + LANES] = message[at : at + rows, :]


def first_kernel(places, mine, other, inverse_out, message, work, schur, carried, inverse, *, pieces, half):
    work[...] = jnp.zeros(work.shape, jnp.float32)
    unpack(places, mine, other, message, pieces, half, 0, work)
    factor_block(work, inverse_out, schur, carried, inverse)


def second_kernel(
    places, mine, other, inverse_first, lower_out, inverse_out, message, work, schur, carried, inverse, *, pieces, half
):
    full = lax.Precision.HIGHEST
    unpack(places, mine, other, message, pieces, half, 1, work)
    lower_out[...] = dot_nt(work[...], inverse_first[...], full)
    unpack(places, mine, other, message, pieces, half, 2, work)
    work[...] = work[...] - dot_nt(lower_out[...], lower_out[...], full)
    factor_block(work, inverse_out, schur, carried, inverse)


def scratch(block, total):
    small = pltpu.VMEM((LANES, LANES), jnp.float32)
    return [pltpu.VMEM((total, LANES), jnp.float32), pltpu.VMEM((block, block), jnp.float32), small, small, small]


def pivot_specs(count):
    return [pl.BlockSpec(memory_space=pltpu.SMEM)] + [pl.BlockSpec(memory_space=pltpu.VMEM)] * count


def first_inverse(places, mine, other, block):
    pieces, total = strips(block)
    square = jax.ShapeDtypeStruct((block, block), jnp.float32)
    return pl.pallas_call(
        lambda *refs: first_kernel(*refs, pieces=pieces, half=total // 2),
        out_shape=square,
        in_specs=pivot_specs(2),
        scratch_shapes=scratch(block, total),
        name="first",
    )(places, mine, other)


def second_inverse(places, mine, other, inverse_first, block):
    pieces, total = strips(block)
    square = jax.ShapeDtypeStruct((block, block), jnp.float32)
    return pl.pallas_call(
        lambda *refs: second_kernel(*refs, pieces=pieces, half=total // 2),
        out_shape=(square, square),
        in_specs=pivot_specs(3),
        scratch_shapes=scratch(block, total),
        name="second",
    )(places, mine, other, inverse_first)


def split(value):
    high = value.astype(jnp.bfloat16)
    return high, (value - high.astype(jnp.float32)).astype(jnp.bfloat16)


def three(left, right):
    def one(a, b):
        return lax.dot_general(a, b, (((1,), (0,)), ((), ())), preferred_element_type=jnp.float32)

    return one(left[0], right[0]) + (one(left[0], right[1]) + one(left[1], right[0]))


def tail_kernel(
    places, pattern, row_order, col_order, inverse0, lower, inverse1, mine, other, matrix, *rest, block, tall, broad, chunks
):
    arrived = rest[: len(rest) - 13]
    out, current, panel, slab, full, left_high, left_low, right_high, right_low, in_sems, panel_sems, slab_sems, out_sems = rest[
        len(rest) - 13 :
    ]
    exact = lax.Precision.HIGHEST
    side = places[PLACE_SIDE]
    half = tall * block // 2
    size = block // chunks
    for s in range(2):
        low = pl.multiple_of(side * half, 8)
        high = pl.multiple_of((1 - side) * half, 8)
        pltpu.make_async_copy(mine.at[s], panel.at[s, pl.ds(low, half), :], panel_sems.at[s, 0]).start()
        pltpu.make_async_copy(other.at[s], panel.at[s, pl.ds(high, half), :], panel_sems.at[s, 1]).start()
    for s in range(2):
        distance = places[DISTANCE + s]
        for k in range(chunks):
            target = slab.at[s, pl.ds(k * size, size), :]

            @pl.when(distance == 0)
            def _():
                source = matrix.at[pl.ds(pl.multiple_of(places[TOP + s] + k * size, 8), size), :]
                pltpu.make_async_copy(source, target, slab_sems.at[s, k]).start()

            for d in range(1, len(arrived) - chunks + 2):

                @pl.when(distance == d)
                def _():
                    pltpu.make_async_copy(arrived[k + d - 1].at[s], target, slab_sems.at[s, k]).start()

    for t in range(tall):
        rows = pl.ds(t * block, block)
        pltpu.make_async_copy(matrix.at[rows, :], current.at[rows, :], in_sems.at[t]).start()
    for s in range(2):
        pltpu.make_async_copy(mine.at[s], panel.at[s, pl.ds(0, half), :], panel_sems.at[s, 0]).wait()
        pltpu.make_async_copy(other.at[s], panel.at[s, pl.ds(0, half), :], panel_sems.at[s, 1]).wait()

    row_ids = [row_order[places[ROW] * tall + t] for t in range(tall)]
    col_ids = [col_order[places[COL] * broad + u] for u in range(broad)]
    zeros = jnp.zeros((block, block), jnp.bfloat16)
    for t in range(tall):
        rows = slice(t * block, (t + 1) * block)
        for s in range(2):
            lanes = slice(s * block, (s + 1) * block)
            linked = pattern[row_ids[t], s] == 1
            used = linked & (row_ids[t] > s)

            @pl.when(linked)
            def _():
                if s == 0:
                    value = dot_nt(panel[0, rows, :], inverse0[...], exact)
                else:
                    value = panel[1, rows, :] - dot_nt(full[0, rows, :], lower[...], exact)
                    value = dot_nt(value, inverse1[...], exact)
                full[s, rows, :] = value
                high, low = split(value)
                left_high[rows, lanes] = high
                left_low[rows, lanes] = low

            @pl.when(jnp.logical_not(used))
            def _():
                left_high[rows, lanes] = zeros
                left_low[rows, lanes] = zeros
                if s == 0:

                    @pl.when(jnp.logical_not(linked))
                    def _():
                        full[0, rows, :] = jnp.zeros((block, block), jnp.float32)

    for s in range(2):
        for k in range(chunks):
            target = slab.at[s, pl.ds(k * size, size), :]
            pltpu.make_async_copy(matrix.at[pl.ds(0, size), :], target, slab_sems.at[s, k]).wait()
    for u in range(broad):
        lanes = slice(u * block, (u + 1) * block)
        for s in range(2):
            rows = slice(s * block, (s + 1) * block)
            used = (pattern[col_ids[u], s] == 1) & (col_ids[u] > s)

            @pl.when(used)
            def _():
                if s == 0:
                    value = dot_nn(inverse0[...], slab[0, :, lanes], exact)
                    slab[0, :, lanes] = value
                else:
                    value = slab[1, :, lanes] - dot_nn(lower[...], slab[0, :, lanes], exact)
                    value = dot_nn(inverse1[...], value, exact)
                high, low = split(value)
                right_high[rows, lanes] = high
                right_low[rows, lanes] = low

            @pl.when(jnp.logical_not(used))
            def _():
                right_high[rows, lanes] = zeros
                right_low[rows, lanes] = zeros
                if s == 0:
                    slab[0, :, lanes] = jnp.zeros((block, block), jnp.float32)

    triangle = lax.broadcasted_iota(jnp.int32, (block, block), 0) >= lax.broadcasted_iota(jnp.int32, (block, block), 1)
    for t in range(tall):
        rows = slice(t * block, (t + 1) * block)
        whole = pl.ds(t * block, block)
        pltpu.make_async_copy(matrix.at[whole, :], current.at[whole, :], in_sems.at[t]).wait()
        for u in range(broad):
            lanes = slice(u * block, (u + 1) * block)
            retained = (pattern[row_ids[t], col_ids[u]] == 1) & (row_ids[t] >= col_ids[u])

            @pl.when(retained & (col_ids[u] >= 2))
            def _():
                left = left_high[rows, :], left_low[rows, :]
                right = right_high[:, lanes], right_low[:, lanes]
                current[rows, lanes] = current[rows, lanes] - three(left, right)

            for s in range(2):

                @pl.when(retained & (col_ids[u] == s))
                def _():
                    value = full[s, rows, :]
                    current[rows, lanes] = jnp.where(triangle | (row_ids[t] != s), value, 0.0)

            @pl.when(jnp.logical_not(retained))
            def _():
                current[rows, lanes] = jnp.zeros((block, block), jnp.float32)

        pltpu.make_async_copy(current.at[whole, :], out.at[whole, :], out_sems.at[t]).start()
    for t in range(tall):
        whole = pl.ds(t * block, block)
        pltpu.make_async_copy(current.at[whole, :], out.at[whole, :], out_sems.at[t]).wait()


def tail(places, pattern, row_order, col_order, inverse0, lower, inverse1, mine, other, matrix, arrived, block):
    local_rows, width = matrix.shape
    tall, broad = local_rows // block, width // block
    smem = pl.BlockSpec(memory_space=pltpu.SMEM)
    vmem = pl.BlockSpec(memory_space=pltpu.VMEM)
    hbm = pl.BlockSpec(memory_space=pl.ANY)
    dma = pltpu.SemaphoreType.DMA
    return pl.pallas_call(
        lambda *refs: tail_kernel(*refs, block=block, tall=tall, broad=broad, chunks=CHUNKS),
        out_shape=jax.ShapeDtypeStruct(matrix.shape, matrix.dtype),
        in_specs=[smem] * 4 + [vmem] * 3 + [hbm] * (3 + len(arrived)),
        out_specs=hbm,
        scratch_shapes=[
            pltpu.VMEM((local_rows, width), jnp.float32),
            pltpu.VMEM((2, local_rows, block), jnp.float32),
            pltpu.VMEM((2, block, width), jnp.float32),
            pltpu.VMEM((2, local_rows, block), jnp.float32),
            pltpu.VMEM((local_rows, 2 * block), jnp.bfloat16),
            pltpu.VMEM((local_rows, 2 * block), jnp.bfloat16),
            pltpu.VMEM((2 * block, width), jnp.bfloat16),
            pltpu.VMEM((2 * block, width), jnp.bfloat16),
            dma((tall,)),
            dma((2, 2)),
            dma((2, CHUNKS)),
            dma((tall,)),
        ],
        name="tail",
    )(places, pattern, row_order, col_order, inverse0, lower, inverse1, mine, other, matrix, *arrived)


ROOT_ROW, ROOT_COL, TOP, EDGE, DISTANCE, ROW, COL, PLACE_SIDE = 0, 2, 4, 6, 8, 10, 11, 12


def find_places(row_order, col_order, rows, block, tall, broad):
    indices = jnp.arange(row_order.shape[0], dtype=jnp.int32)
    orders = jnp.stack([row_order, col_order])
    wanted = jnp.arange(2, dtype=jnp.int32)
    found = jnp.sum(jnp.where(orders[:, None, :] == wanted[None, :, None], indices, 0), axis=2)
    row, col = lax.axis_index("row"), lax.axis_index("col")
    per = jnp.array([[tall], [broad]], jnp.int32)
    roots = found // per
    offsets = found % per * block
    distance = (row - roots[0] + rows) % rows
    here = jnp.stack([row, col, col & 1])
    return jnp.concatenate([roots.reshape(-1), offsets.reshape(-1), distance, here])


def exchange(value, axis, pairs):
    return lax.ppermute(value, axis, pairs)


def plane_pairs(cols, step):
    bits = [1 << b for b in range(1, cols.bit_length() - 1)]
    turn = len(bits) // 2
    first, second = bits[step], (bits[turn:] + bits[:turn])[step]
    return [(i, i ^ (second if i & 1 else first)) for i in range(cols)], first, second


def make_body(rows, cols):
    plane_steps = cols.bit_length() - 2
    core_pairs = [(i, i ^ 1) for i in range(cols)]
    ring = [(i, (i + 1) % rows) for i in range(rows)]

    def body(matrix, pattern, row_order, col_order):
        local_rows, width = matrix.shape
        total = row_order.shape[0]
        block = local_rows * rows // total
        tall, broad = local_rows // block, width // block
        places = find_places(row_order, col_order, rows, block, tall, broad)
        row, col, side = places[ROW], places[COL], places[PLACE_SIDE]
        root_row = [places[ROOT_ROW + s] for s in range(2)]
        root_col = [places[ROOT_COL + s] for s in range(2)]

        pieces, packed = strips(block)
        tiles = block // LANES
        bounds = [tiles * (tiles + 1) // 2 * LANES, tiles * (tiles + 1) // 2 * LANES + block * block // LANES]

        def choose(start, value, differs_first, differs_second, received, axis):
            at = start + lax.broadcasted_iota(jnp.int32, value.shape, 0)
            if axis == "col":
                cut, cut_flags = bounds[1], (differs_first, differs_second)
            else:
                cut, cut_flags = bounds[0], (differs_first, differs_second)
            return jnp.where(jnp.where(at < cut, cut_flags[0], cut_flags[1]), received, value)

        keep, send = pack(places, matrix, block)
        received = exchange(send, "col", core_pairs)
        size = packed // 2
        start = side * size
        value = choose(start, keep, *[((root_col[s] ^ col) & 1) != 0 for s in range(2)], received, "col")
        path = []
        for step in range(plane_steps):
            pairs, first, second = plane_pairs(cols, step)
            bit = jnp.where(side == 0, first, second)
            upper = (col & bit) != 0
            size = size // 2
            low, high = value[:size], value[size:]
            received = exchange(jnp.where(upper, low, high), "col", pairs)
            start = start + jnp.where(upper, size, 0)
            flags = [((root_col[s] ^ col) & bit) != 0 for s in range(2)]
            value = choose(start, jnp.where(upper, high, low), *flags, received, "col")
            path.append((pairs, upper))
        for b in range(rows.bit_length() - 1):
            received = exchange(value, "row", [(i, i ^ (1 << b)) for i in range(rows)])
            flags = [((root_row[s] ^ row) & (1 << b)) != 0 for s in range(2)]
            value = choose(start, value, *flags, received, "row")
        for pairs, upper in path[::-1]:
            received = exchange(value, "col", pairs)
            value = jnp.concatenate([jnp.where(upper, received, value), jnp.where(upper, value, received)], axis=0)
        mine = value
        other = exchange(mine, "col", core_pairs)

        arrived = []
        chunk = block // CHUNKS
        for step in range(CHUNKS + rows - 2):
            parts = []
            for s in range(2):
                at = places[TOP + s] + min(step, CHUNKS - 1) * chunk
                own = lax.dynamic_slice(matrix, (at, 0), (chunk, width))
                if step:
                    own = jnp.where(places[DISTANCE + s] == 0, own, arrived[-1][s])
                parts.append(own)
            arrived.append(exchange(jnp.stack(parts), "row", ring))

        half = local_rows // 2

        def halves(which):
            return jnp.stack(
                [lax.dynamic_slice(matrix, (which * half, places[EDGE + s]), (half, block)) for s in range(2)]
            )

        def pick(flags, received, value):
            return jnp.where(jnp.stack(flags)[:, None, None], received, value)

        received = exchange(halves(1 - side), "col", core_pairs)
        panel = pick([((root_col[s] ^ col) & 1) != 0 for s in range(2)], received, halves(side))
        for step in range(plane_steps):
            pairs, first, second = plane_pairs(cols, step)
            bit = jnp.where(side == 0, first, second)
            received = exchange(panel, "col", pairs)
            panel = pick([((root_col[s] ^ col) & bit) != 0 for s in range(2)], received, panel)
        panel_other = exchange(panel, "col", core_pairs)

        inverse0 = first_inverse(places, mine, other, block)
        lower, inverse1 = second_inverse(places, mine, other, inverse0, block)
        return tail(
            places, pattern, row_order, col_order, inverse0, lower, inverse1, panel, panel_other, matrix, arrived, block
        )

    return body


def solution(mesh):
    in_specs = (P("row", "col"), P(), P(), P())
    out_specs = P("row", "col")
    body = make_body(mesh.shape["row"], mesh.shape["col"])
    return jax.shard_map(body, mesh=mesh, in_specs=in_specs, out_specs=out_specs, check_vma=False)
```

```python
import jax
import jax.numpy as jnp
from jax import lax
from jax.experimental import pallas as pl
from jax.experimental.pallas import tpu as pltpu
from jax.sharding import PartitionSpec as P

LANES = 128
CHUNKS = 2


def dot_nt(a, b, precision):
    dims = (((1,), (1,)), ((), ()))
    return lax.dot_general(a, b, dims, precision=precision, preferred_element_type=jnp.float32)


def dot_nn(a, b, precision):
    dims = (((1,), (0,)), ((), ()))
    return lax.dot_general(a, b, dims, precision=precision, preferred_element_type=jnp.float32)


def unit(size):
    rows = lax.broadcasted_iota(jnp.int32, (size, size), 0)
    lanes = lax.broadcasted_iota(jnp.int32, (size, size), 1)
    return (rows == lanes).astype(jnp.float32)


def invert_diagonal(schur, carried, inverse):
    tile = (8, LANES)
    sublane = lax.broadcasted_iota(jnp.int32, tile, 0)
    carried[...] = unit(LANES)

    def row_of(x, p):
        return jnp.broadcast_to(x[p : p + 1, :], tile)

    def lane_of(x, p):
        return jnp.broadcast_to(x[:, p : p + 1], tile)

    steps = LANES // 8
    for b in range(steps):
        rows = schur[8 * b : 8 * b + 8, :]
        extra = carried[8 * b : 8 * b + 8, :]
        columns = [lane_of(rows, 8 * b + p) for p in range(8)]
        reciprocals = jnp.zeros(tile, jnp.float32)
        pivots = jnp.ones(tile, jnp.float32)
        for p in range(8):
            pivot = row_of(columns[p], p)
            reciprocal = 1.0 / pivot
            factor = jnp.where(sublane > p, columns[p] * reciprocal, 0.0)
            for q in range(p + 1, 8):
                columns[q] = columns[q] - factor * row_of(columns[q], p)
            rows = rows - factor * row_of(rows, p)
            extra = extra - factor * row_of(extra, p)
            reciprocals = jnp.where(sublane == p, reciprocal, reciprocals)
            pivots = jnp.where(sublane == p, pivot, pivots)
        inverse[8 * b : 8 * b + 8, :] = extra * lax.rsqrt(pivots)
        if b == steps - 1:
            break
        solved = rows * reciprocals
        solved_extra = extra * reciprocals
        for p in range(7, 0, -1):
            factor = jnp.where(sublane < p, columns[p] * reciprocals, 0.0)
            solved = solved - factor * row_of(solved, p)
            solved_extra = solved_extra - factor * row_of(solved_extra, p)
        right = [row_of(solved, p) for p in range(8)]
        right_extra = [row_of(solved_extra, p) for p in range(8)]
        for i in range(b + 1, steps):
            part = schur[8 * i : 8 * i + 8, :]
            part_extra = carried[8 * i : 8 * i + 8, :]
            left = [lane_of(part, 8 * b + p) for p in range(8)]
            for p in range(8):
                part = part - left[p] * right[p]
                part_extra = part_extra - left[p] * right_extra[p]
            schur[8 * i : 8 * i + 8, :] = part
            carried[8 * i : 8 * i + 8, :] = part_extra


def factor_block(work, out, schur, carried, inverse):
    size = work.shape[0]
    out[...] = unit(size)
    steps = size // LANES
    full = lax.Precision.HIGHEST

    def step(k, carry):
        low = pl.multiple_of(k * LANES, LANES)
        schur[...] = work[pl.ds(low, LANES), pl.ds(low, LANES)]
        invert_diagonal(schur, carried, inverse)
        out[pl.ds(low, LANES), :] = dot_nn(inverse[...], out[pl.ds(low, LANES), :], full)
        for done in range(steps - 1):

            @pl.when(k == done)
            def _():
                top, edge = done * LANES, (done + 1) * LANES
                panel = dot_nt(work[edge:, top:edge], inverse[...], full)
                work[edge:, edge:] = work[edge:, edge:] - dot_nt(panel, panel, full)
                out[edge:, :edge] = out[edge:, :edge] - dot_nn(panel, out[top:edge, :edge], full)

        return carry

    lax.fori_loop(0, steps, step, 0)


def strips(block):
    tiles = block // LANES
    found, low = [], 0
    for part in range(3):
        for lane in range(tiles):
            first = 0 if part == 1 else lane * LANES
            found.append([part, first, lane * LANES, block - first, low])
            low += block - first
    half = low // 2
    split = []
    for part, first, lane, rows, at in found:
        cut = half - at
        if 0 < cut < rows:
            split.append((part, first, lane, cut, at))
            split.append((part, first + cut, lane, rows - cut, half))
        else:
            split.append((part, first, lane, rows, at))
    return split, low


def pack_kernel(here, row_order, col_order, matrix, places, keep, send, sems, *, block, tall, broad, rows, pieces, half):
    for axis, (order, per) in enumerate(((row_order, tall), (col_order, broad))):
        first = jnp.int32(0)
        second = jnp.int32(0)
        for i in range(order.shape[0]):
            first = jnp.where(order[i] == 0, i, first)
            second = jnp.where(order[i] == 1, i, second)
        for s, found in enumerate((first, second)):
            places[(ROOT_ROW, ROOT_COL)[axis] + s] = found // per
            places[(TOP, EDGE)[axis] + s] = found % per * block
    for s in range(2):
        places[DISTANCE + s] = (here[0] - places[ROOT_ROW + s] + rows) % rows
    places[ROW] = here[0]
    places[COL] = here[1]
    places[PLACE_SIDE] = here[1] % 2
    for side in range(2):

        @pl.when(here[1] % 2 == side)
        def _():
            for n, (part, first, lane, count, at) in enumerate(pieces):
                row = pl.multiple_of(places[TOP + min(part, 1)] + first, 8)
                column = pl.multiple_of(places[EDGE + part // 2] + lane, LANES)
                target = keep if at // half == side else send
                source = matrix.at[pl.ds(row, count), pl.ds(column, LANES)]
                pltpu.make_async_copy(source, target.at[pl.ds(at % half, count), :], sems.at[n]).start()
            for n, (part, first, lane, count, at) in enumerate(pieces):
                target = keep if at // half == side else send
                source = matrix.at[pl.ds(0, count), pl.ds(0, LANES)]
                pltpu.make_async_copy(source, target.at[pl.ds(at % half, count), :], sems.at[n]).wait()


def pack(row_order, col_order, matrix, block, rows):
    pieces, total = strips(block)
    half = total // 2
    out = jax.ShapeDtypeStruct((half, LANES), jnp.float32)
    smem = pl.BlockSpec(memory_space=pltpu.SMEM)
    vmem = pl.BlockSpec(memory_space=pltpu.VMEM)
    here = jnp.stack([lax.axis_index("row"), lax.axis_index("col")])
    sizes = dict(block=block, tall=matrix.shape[0] // block, broad=matrix.shape[1] // block, rows=rows)
    return pl.pallas_call(
        lambda *refs: pack_kernel(*refs, pieces=pieces, half=half, **sizes),
        out_shape=(jax.ShapeDtypeStruct((13,), jnp.int32), out, out),
        in_specs=[smem] * 3 + [pl.BlockSpec(memory_space=pl.ANY)],
        out_specs=(smem, vmem, vmem),
        scratch_shapes=[pltpu.SemaphoreType.DMA((len(pieces),))],
        name="pack",
    )(here, row_order, col_order, matrix)


def unpack(places, mine, other, message, pieces, half, wanted, work):
    side = places[PLACE_SIDE]
    message[pl.ds(pl.multiple_of(side * half, 8), half), :] = mine[...]
    message[pl.ds(pl.multiple_of((1 - side) * half, 8), half), :] = other[...]
    for part, first, lane, rows, at in pieces:
        if part == wanted:
            work[first : first + rows, lane : lane + LANES] = message[at : at + rows, :]


def first_kernel(places, mine, other, inverse_out, message, work, schur, carried, inverse, *, pieces, half):
    work[...] = jnp.zeros(work.shape, jnp.float32)
    unpack(places, mine, other, message, pieces, half, 0, work)
    factor_block(work, inverse_out, schur, carried, inverse)


def second_kernel(
    places, mine, other, inverse_first, lower_out, inverse_out, message, work, schur, carried, inverse, *, pieces, half
):
    full = lax.Precision.HIGHEST
    unpack(places, mine, other, message, pieces, half, 1, work)
    lower_out[...] = dot_nt(work[...], inverse_first[...], full)
    unpack(places, mine, other, message, pieces, half, 2, work)
    work[...] = work[...] - dot_nt(lower_out[...], lower_out[...], full)
    factor_block(work, inverse_out, schur, carried, inverse)


def scratch(block, total):
    small = pltpu.VMEM((LANES, LANES), jnp.float32)
    return [pltpu.VMEM((total, LANES), jnp.float32), pltpu.VMEM((block, block), jnp.float32), small, small, small]


def pivot_specs(count):
    return [pl.BlockSpec(memory_space=pltpu.SMEM)] + [pl.BlockSpec(memory_space=pltpu.VMEM)] * count


def first_inverse(places, mine, other, block):
    pieces, total = strips(block)
    square = jax.ShapeDtypeStruct((block, block), jnp.float32)
    return pl.pallas_call(
        lambda *refs: first_kernel(*refs, pieces=pieces, half=total // 2),
        out_shape=square,
        in_specs=pivot_specs(2),
        scratch_shapes=scratch(block, total),
        name="first",
    )(places, mine, other)


def second_inverse(places, mine, other, inverse_first, block):
    pieces, total = strips(block)
    square = jax.ShapeDtypeStruct((block, block), jnp.float32)
    return pl.pallas_call(
        lambda *refs: second_kernel(*refs, pieces=pieces, half=total // 2),
        out_shape=(square, square),
        in_specs=pivot_specs(3),
        scratch_shapes=scratch(block, total),
        name="second",
    )(places, mine, other, inverse_first)


def split(value):
    high = value.astype(jnp.bfloat16)
    return high, (value - high.astype(jnp.float32)).astype(jnp.bfloat16)


def three(left, right):
    def one(a, b):
        return lax.dot_general(a, b, (((1,), (0,)), ((), ())), preferred_element_type=jnp.float32)

    return one(left[0], right[0]) + (one(left[0], right[1]) + one(left[1], right[0]))


def tail_kernel(
    places, pattern, row_order, col_order, inverse0, lower, inverse1, mine, other, matrix, *rest, block, tall, broad, chunks
):
    arrived = rest[: len(rest) - 13]
    out, current, panel, slab, full, left_high, left_low, right_high, right_low, in_sems, panel_sems, slab_sems, out_sems = rest[
        len(rest) - 13 :
    ]
    exact = lax.Precision.HIGHEST
    side = places[PLACE_SIDE]
    half = tall * block // 2
    size = block // chunks
    for s in range(2):
        low = pl.multiple_of(side * half, 8)
        high = pl.multiple_of((1 - side) * half, 8)
        pltpu.make_async_copy(mine.at[s], panel.at[s, pl.ds(low, half), :], panel_sems.at[s, 0]).start()
        pltpu.make_async_copy(other.at[s], panel.at[s, pl.ds(high, half), :], panel_sems.at[s, 1]).start()
    for s in range(2):
        distance = places[DISTANCE + s]
        for k in range(chunks):
            target = slab.at[s, pl.ds(k * size, size), :]

            @pl.when(distance == 0)
            def _():
                source = matrix.at[pl.ds(pl.multiple_of(places[TOP + s] + k * size, 8), size), :]
                pltpu.make_async_copy(source, target, slab_sems.at[s, k]).start()

            for d in range(1, len(arrived) - chunks + 2):

                @pl.when(distance == d)
                def _():
                    pltpu.make_async_copy(arrived[k + d - 1].at[s], target, slab_sems.at[s, k]).start()

    for t in range(tall):
        rows = pl.ds(t * block, block)
        pltpu.make_async_copy(matrix.at[rows, :], current.at[rows, :], in_sems.at[t]).start()
    for s in range(2):
        pltpu.make_async_copy(mine.at[s], panel.at[s, pl.ds(0, half), :], panel_sems.at[s, 0]).wait()
        pltpu.make_async_copy(other.at[s], panel.at[s, pl.ds(0, half), :], panel_sems.at[s, 1]).wait()

    row_ids = [row_order[places[ROW] * tall + t] for t in range(tall)]
    col_ids = [col_order[places[COL] * broad + u] for u in range(broad)]
    zeros = jnp.zeros((block, block), jnp.bfloat16)
    for t in range(tall):
        rows = slice(t * block, (t + 1) * block)
        for s in range(2):
            lanes = slice(s * block, (s + 1) * block)
            linked = pattern[row_ids[t], s] == 1
            used = linked & (row_ids[t] > s)

            @pl.when(linked)
            def _():
                if s == 0:
                    value = dot_nt(panel[0, rows, :], inverse0[...], exact)
                else:
                    value = panel[1, rows, :] - dot_nt(full[0, rows, :], lower[...], exact)
                    value = dot_nt(value, inverse1[...], exact)
                full[s, rows, :] = value
                high, low = split(value)
                left_high[rows, lanes] = high
                left_low[rows, lanes] = low

            @pl.when(jnp.logical_not(used))
            def _():
                left_high[rows, lanes] = zeros
                left_low[rows, lanes] = zeros
                if s == 0:

                    @pl.when(jnp.logical_not(linked))
                    def _():
                        full[0, rows, :] = jnp.zeros((block, block), jnp.float32)

    for s in range(2):
        for k in range(chunks):
            target = slab.at[s, pl.ds(k * size, size), :]
            pltpu.make_async_copy(matrix.at[pl.ds(0, size), :], target, slab_sems.at[s, k]).wait()
    for u in range(broad):
        lanes = slice(u * block, (u + 1) * block)
        for s in range(2):
            rows = slice(s * block, (s + 1) * block)
            used = (pattern[col_ids[u], s] == 1) & (col_ids[u] > s)

            @pl.when(used)
            def _():
                if s == 0:
                    value = dot_nn(inverse0[...], slab[0, :, lanes], exact)
                    slab[0, :, lanes] = value
                else:
                    value = slab[1, :, lanes] - dot_nn(lower[...], slab[0, :, lanes], exact)
                    value = dot_nn(inverse1[...], value, exact)
                high, low = split(value)
                right_high[rows, lanes] = high
                right_low[rows, lanes] = low

            @pl.when(jnp.logical_not(used))
            def _():
                right_high[rows, lanes] = zeros
                right_low[rows, lanes] = zeros
                if s == 0:
                    slab[0, :, lanes] = jnp.zeros((block, block), jnp.float32)

    triangle = lax.broadcasted_iota(jnp.int32, (block, block), 0) >= lax.broadcasted_iota(jnp.int32, (block, block), 1)
    for t in range(tall):
        rows = slice(t * block, (t + 1) * block)
        whole = pl.ds(t * block, block)
        pltpu.make_async_copy(matrix.at[whole, :], current.at[whole, :], in_sems.at[t]).wait()
        for u in range(broad):
            lanes = slice(u * block, (u + 1) * block)
            retained = (pattern[row_ids[t], col_ids[u]] == 1) & (row_ids[t] >= col_ids[u])

            @pl.when(retained & (col_ids[u] >= 2))
            def _():
                left = left_high[rows, :], left_low[rows, :]
                right = right_high[:, lanes], right_low[:, lanes]
                current[rows, lanes] = current[rows, lanes] - three(left, right)

            for s in range(2):

                @pl.when(retained & (col_ids[u] == s))
                def _():
                    value = full[s, rows, :]
                    current[rows, lanes] = jnp.where(triangle | (row_ids[t] != s), value, 0.0)

            @pl.when(jnp.logical_not(retained))
            def _():
                current[rows, lanes] = jnp.zeros((block, block), jnp.float32)

        pltpu.make_async_copy(current.at[whole, :], out.at[whole, :], out_sems.at[t]).start()
    for t in range(tall):
        whole = pl.ds(t * block, block)
        pltpu.make_async_copy(current.at[whole, :], out.at[whole, :], out_sems.at[t]).wait()


def tail(places, pattern, row_order, col_order, inverse0, lower, inverse1, mine, other, matrix, arrived, block):
    local_rows, width = matrix.shape
    tall, broad = local_rows // block, width // block
    smem = pl.BlockSpec(memory_space=pltpu.SMEM)
    vmem = pl.BlockSpec(memory_space=pltpu.VMEM)
    hbm = pl.BlockSpec(memory_space=pl.ANY)
    dma = pltpu.SemaphoreType.DMA
    return pl.pallas_call(
        lambda *refs: tail_kernel(*refs, block=block, tall=tall, broad=broad, chunks=CHUNKS),
        out_shape=jax.ShapeDtypeStruct(matrix.shape, matrix.dtype),
        in_specs=[smem] * 4 + [vmem] * 3 + [hbm] * (3 + len(arrived)),
        out_specs=hbm,
        scratch_shapes=[
            pltpu.VMEM((local_rows, width), jnp.float32),
            pltpu.VMEM((2, local_rows, block), jnp.float32),
            pltpu.VMEM((2, block, width), jnp.float32),
            pltpu.VMEM((2, local_rows, block), jnp.float32),
            pltpu.VMEM((local_rows, 2 * block), jnp.bfloat16),
            pltpu.VMEM((local_rows, 2 * block), jnp.bfloat16),
            pltpu.VMEM((2 * block, width), jnp.bfloat16),
            pltpu.VMEM((2 * block, width), jnp.bfloat16),
            dma((tall,)),
            dma((2, 2)),
            dma((2, CHUNKS)),
            dma((tall,)),
        ],
        name="tail",
    )(places, pattern, row_order, col_order, inverse0, lower, inverse1, mine, other, matrix, *arrived)


ROOT_ROW, ROOT_COL, TOP, EDGE, DISTANCE, ROW, COL, PLACE_SIDE = 0, 2, 4, 6, 8, 10, 11, 12


def barrier(*values):
    return lax.optimization_barrier(values)


def exchange(value, axis, pairs):
    return lax.ppermute(value, axis, pairs)


def plane_pairs(cols, step):
    bits = [1 << b for b in range(1, cols.bit_length() - 1)]
    turn = len(bits) // 2
    first, second = bits[step], (bits[turn:] + bits[:turn])[step]
    return [(i, i ^ (second if i & 1 else first)) for i in range(cols)], first, second


def make_body(rows, cols):
    plane_steps = cols.bit_length() - 2
    core_pairs = [(i, i ^ 1) for i in range(cols)]
    ring = [(i, (i + 1) % rows) for i in range(rows)]

    def body(matrix, pattern, row_order, col_order):
        local_rows, width = matrix.shape
        total = row_order.shape[0]
        block = local_rows * rows // total
        tall, broad = local_rows // block, width // block
        pieces, packed = strips(block)
        tiles = block // LANES
        places, keep, send = pack(row_order, col_order, matrix, block, rows)
        row, col, side = places[ROW], places[COL], places[PLACE_SIDE]
        root_row = [places[ROOT_ROW + s] for s in range(2)]
        root_col = [places[ROOT_COL + s] for s in range(2)]
        corner = tiles * (tiles + 1) // 2 * LANES
        bounds = [corner, corner + tiles * tiles * LANES]

        def choose(start, value, flags, received, bound):
            at = start + lax.broadcasted_iota(jnp.int32, value.shape, 0)
            return jnp.where(jnp.where(at < bound, flags[0], flags[1]), received, value)

        chunk = block // CHUNKS

        def ring_payload(step, arrived):
            parts = []
            for s in range(2):
                at = places[TOP + s] + min(step, CHUNKS - 1) * chunk
                own = lax.dynamic_slice(matrix, (at, 0), (chunk, width))
                if step:
                    own = jnp.where(places[DISTANCE + s] == 0, own, arrived[s])
                parts.append(own)
            return jnp.stack(parts)

        half = local_rows // 2

        def halves(which):
            return jnp.stack(
                [lax.dynamic_slice(matrix, (which * half, places[EDGE + s]), (half, block)) for s in range(2)]
            )

        def pick(bit, received, value):
            flags = [((root_col[s] ^ col) & bit) != 0 for s in range(2)]
            return jnp.where(jnp.stack(flags)[:, None, None], received, value)

        def plane_bit(step):
            pairs, first, second = plane_pairs(cols, step)
            return pairs, jnp.where(side == 0, first, second)

        received = exchange(send, "col", core_pairs)
        size = packed // 2
        start = side * size
        value = choose(start, keep, [((root_col[s] ^ col) & 1) != 0 for s in range(2)], received, bounds[1])
        value, ring_now, panel_send = barrier(value, ring_payload(0, None), halves(1 - side))
        arrived = [exchange(ring_now, "row", ring)]
        panel_received = exchange(panel_send, "col", core_pairs)
        path = []
        for step in range(plane_steps):
            pairs, bit = plane_bit(step)
            upper = (col & bit) != 0
            size = size // 2
            low, high = value[:size], value[size:]
            received = exchange(jnp.where(upper, low, high), "col", pairs)
            start = start + jnp.where(upper, size, 0)
            flags = [((root_col[s] ^ col) & bit) != 0 for s in range(2)]
            value = choose(start, jnp.where(upper, high, low), flags, received, bounds[1])
            path.append((pairs, upper))
        panel = pick(1, panel_received, halves(side))
        for b in range(rows.bit_length() - 1):
            received = exchange(value, "row", [(i, i ^ (1 << b)) for i in range(rows)])
            flags = [((root_row[s] ^ row) & (1 << b)) != 0 for s in range(2)]
            value = choose(start, value, flags, received, bounds[0])
        value, panel, ring_now = barrier(value, panel, ring_payload(1, arrived[-1]))
        arrived.append(exchange(ring_now, "row", ring))
        for pairs, upper in path[::-1]:
            received = exchange(value, "col", pairs)
            value = jnp.concatenate([jnp.where(upper, received, value), jnp.where(upper, value, received)], axis=0)
        mine = value
        other = exchange(mine, "col", core_pairs)

        last = CHUNKS + rows - 2
        mine, other, panel, ring_now = barrier(mine, other, panel, ring_payload(2, arrived[-1]))
        arrived.append(exchange(ring_now, "row", ring))
        pairs, bit = plane_bit(0)
        received = exchange(panel, "col", pairs)
        inverse0 = first_inverse(places, mine, other, block)
        panel = pick(bit, received, panel)
        inverse0, panel, ring_now = barrier(inverse0, panel, ring_payload(3, arrived[-1]))
        arrived.append(exchange(ring_now, "row", ring))
        for step in range(1, plane_steps):
            pairs, bit = plane_bit(step)
            received = exchange(panel, "col", pairs)
            if step == 1:
                lower, inverse1 = second_inverse(places, mine, other, inverse0, block)
            panel = pick(bit, received, panel)
        lower, inverse1, panel = barrier(lower, inverse1, panel)
        for step in range(4, last):
            arrived.append(exchange(ring_payload(step, arrived[-1]), "row", ring))
        panel_other = exchange(panel, "col", core_pairs)
        return tail(
            places, pattern, row_order, col_order, inverse0, lower, inverse1, panel, panel_other, matrix, arrived, block
        )

    return body


def solution(mesh):
    in_specs = (P("row", "col"), P(), P(), P())
    out_specs = P("row", "col")
    body = make_body(mesh.shape["row"], mesh.shape["col"])
    return jax.shard_map(body, mesh=mesh, in_specs=in_specs, out_specs=out_specs, check_vma=False)
```

```python
import jax
import jax.numpy as jnp
from jax import lax
from jax.experimental import pallas as pl
from jax.experimental.pallas import tpu as pltpu
from jax.sharding import PartitionSpec as P

LANES = 128
CHUNKS = 3


def dot_nt(a, b, precision):
    dims = (((1,), (1,)), ((), ()))
    return lax.dot_general(a, b, dims, precision=precision, preferred_element_type=jnp.float32)


def dot_nn(a, b, precision):
    dims = (((1,), (0,)), ((), ()))
    return lax.dot_general(a, b, dims, precision=precision, preferred_element_type=jnp.float32)


def unit(size):
    rows = lax.broadcasted_iota(jnp.int32, (size, size), 0)
    lanes = lax.broadcasted_iota(jnp.int32, (size, size), 1)
    return (rows == lanes).astype(jnp.float32)


def invert_diagonal(schur, carried, inverse):
    tile = (8, LANES)
    sublane = lax.broadcasted_iota(jnp.int32, tile, 0)
    carried[...] = unit(LANES)

    def row_of(x, p):
        return jnp.broadcast_to(x[p : p + 1, :], tile)

    def lane_of(x, p):
        return jnp.broadcast_to(x[:, p : p + 1], tile)

    steps = LANES // 8
    for b in range(steps):
        rows = schur[8 * b : 8 * b + 8, :]
        extra = carried[8 * b : 8 * b + 8, :]
        columns = [lane_of(rows, 8 * b + p) for p in range(8)]
        reciprocals = jnp.zeros(tile, jnp.float32)
        pivots = jnp.ones(tile, jnp.float32)
        for p in range(8):
            pivot = row_of(columns[p], p)
            reciprocal = 1.0 / pivot
            factor = jnp.where(sublane > p, columns[p] * reciprocal, 0.0)
            for q in range(p + 1, 8):
                columns[q] = columns[q] - factor * row_of(columns[q], p)
            rows = rows - factor * row_of(rows, p)
            extra = extra - factor * row_of(extra, p)
            reciprocals = jnp.where(sublane == p, reciprocal, reciprocals)
            pivots = jnp.where(sublane == p, pivot, pivots)
        inverse[8 * b : 8 * b + 8, :] = extra * lax.rsqrt(pivots)
        if b == steps - 1:
            break
        solved = rows * reciprocals
        solved_extra = extra * reciprocals
        for p in range(7, 0, -1):
            factor = jnp.where(sublane < p, columns[p] * reciprocals, 0.0)
            solved = solved - factor * row_of(solved, p)
            solved_extra = solved_extra - factor * row_of(solved_extra, p)
        right = [row_of(solved, p) for p in range(8)]
        right_extra = [row_of(solved_extra, p) for p in range(8)]
        for i in range(b + 1, steps):
            part = schur[8 * i : 8 * i + 8, :]
            part_extra = carried[8 * i : 8 * i + 8, :]
            left = [lane_of(part, 8 * b + p) for p in range(8)]
            for p in range(8):
                part = part - left[p] * right[p]
                part_extra = part_extra - left[p] * right_extra[p]
            schur[8 * i : 8 * i + 8, :] = part
            carried[8 * i : 8 * i + 8, :] = part_extra


def factor_panels(work, out, schur, carried, inverse, first, last):
    steps = work.shape[0] // LANES
    full = lax.Precision.HIGHEST

    def step(k, carry):
        low = pl.multiple_of(k * LANES, LANES)
        schur[...] = work[pl.ds(low, LANES), pl.ds(low, LANES)]
        invert_diagonal(schur, carried, inverse)
        out[pl.ds(low, LANES), :] = dot_nn(inverse[...], out[pl.ds(low, LANES), :], full)
        for done in range(first, min(last, steps - 1)):

            @pl.when(k == done)
            def _():
                top, edge = done * LANES, (done + 1) * LANES
                panel = dot_nt(work[edge:, top:edge], inverse[...], full)
                work[edge:, edge:] = work[edge:, edge:] - dot_nt(panel, panel, full)
                out[edge:, :edge] = out[edge:, :edge] - dot_nn(panel, out[top:edge, :edge], full)

        return carry

    lax.fori_loop(first, last, step, 0)


def strips(block):
    tiles = block // LANES
    found, low = [], 0
    for part in range(3):
        for lane in range(tiles):
            first = 0 if part == 1 else lane * LANES
            found.append([part, first, lane * LANES, block - first, low])
            low += block - first
    half = low // 2
    split = []
    for part, first, lane, rows, at in found:
        cut = half - at
        if 0 < cut < rows:
            split.append((part, first, lane, cut, at))
            split.append((part, first + cut, lane, rows - cut, half))
        else:
            split.append((part, first, lane, rows, at))
    return split, low


def pack_kernel(here, row_order, col_order, matrix, places, keep, send, sems, *, block, tall, broad, rows, pieces, half):
    for axis, (order, per) in enumerate(((row_order, tall), (col_order, broad))):
        first = jnp.int32(0)
        second = jnp.int32(0)
        for i in range(order.shape[0]):
            first = jnp.where(order[i] == 0, i, first)
            second = jnp.where(order[i] == 1, i, second)
        for s, found in enumerate((first, second)):
            places[(ROOT_ROW, ROOT_COL)[axis] + s] = found // per
            places[(TOP, EDGE)[axis] + s] = found % per * block
    for s in range(2):
        places[DISTANCE + s] = (here[0] - places[ROOT_ROW + s] + rows) % rows
    places[ROW] = here[0]
    places[COL] = here[1]
    places[PLACE_SIDE] = here[1] % 2
    for side in range(2):

        @pl.when(here[1] % 2 == side)
        def _():
            for n, (part, first, lane, count, at) in enumerate(pieces):
                row = pl.multiple_of(places[TOP + min(part, 1)] + first, 8)
                column = pl.multiple_of(places[EDGE + part // 2] + lane, LANES)
                target = keep if at // half == side else send
                source = matrix.at[pl.ds(row, count), pl.ds(column, LANES)]
                pltpu.make_async_copy(source, target.at[pl.ds(at % half, count), :], sems.at[n]).start()
            for n, (part, first, lane, count, at) in enumerate(pieces):
                target = keep if at // half == side else send
                source = matrix.at[pl.ds(0, count), pl.ds(0, LANES)]
                pltpu.make_async_copy(source, target.at[pl.ds(at % half, count), :], sems.at[n]).wait()


def pack(row_order, col_order, matrix, block, rows):
    pieces, total = strips(block)
    half = total // 2
    out = jax.ShapeDtypeStruct((half, LANES), jnp.float32)
    here = jnp.stack([lax.axis_index("row"), lax.axis_index("col")])
    sizes = dict(block=block, tall=matrix.shape[0] // block, broad=matrix.shape[1] // block, rows=rows)
    return pl.pallas_call(
        lambda *refs: pack_kernel(*refs, pieces=pieces, half=half, **sizes),
        out_shape=(jax.ShapeDtypeStruct((13,), jnp.int32), out, out),
        in_specs=[SMEM] * 3 + [ANY],
        out_specs=(SMEM, VMEM, VMEM),
        scratch_shapes=[pltpu.SemaphoreType.DMA((len(pieces),))],
        compiler_params=limit(8),
        name="pack",
    )(here, row_order, col_order, matrix)


def unpack(places, mine, other, message, pieces, half, wanted, work):
    side = places[PLACE_SIDE]
    message[pl.ds(pl.multiple_of(side * half, 8), half), :] = mine[...]
    message[pl.ds(pl.multiple_of((1 - side) * half, 8), half), :] = other[...]
    for part, first, lane, rows, at in pieces:
        if part == wanted:
            work[first : first + rows, lane : lane + LANES] = message[at : at + rows, :]


def first_kernel(places, mine, other, work, out, message, schur, carried, inverse, *, pieces, half, last):
    work[...] = jnp.zeros(work.shape, jnp.float32)
    unpack(places, mine, other, message, pieces, half, 0, work)
    out[...] = unit(work.shape[0])
    factor_panels(work, out, schur, carried, inverse, 0, last)


def second_kernel(places, mine, other, inverse_first, lower, work, out, message, schur, carried, inverse, *, pieces, half, last):
    full = lax.Precision.HIGHEST
    unpack(places, mine, other, message, pieces, half, 1, work)
    lower[...] = dot_nt(work[...], inverse_first[...], full)
    unpack(places, mine, other, message, pieces, half, 2, work)
    work[...] = work[...] - dot_nt(lower[...], lower[...], full)
    out[...] = unit(work.shape[0])
    factor_panels(work, out, schur, carried, inverse, 0, last)


def rest_kernel(work_in, out_in, out, work, schur, carried, inverse, *, first):
    work[...] = work_in[...]
    out[...] = out_in[...]
    factor_panels(work, out, schur, carried, inverse, first, work.shape[0] // LANES)


SMEM = pl.BlockSpec(memory_space=pltpu.SMEM)
VMEM = pl.BlockSpec(memory_space=pltpu.VMEM)
ANY = pl.BlockSpec(memory_space=pl.ANY)
HBM = pl.BlockSpec(memory_space=pltpu.HBM)


def limit(mebibytes):
    return pltpu.CompilerParams(vmem_limit_bytes=mebibytes << 20)


def small(count):
    return [pltpu.VMEM((LANES, LANES), jnp.float32)] * count


def square(block):
    return jax.ShapeDtypeStruct((block, block), jnp.float32)


def start_first(places, mine, other, block, last):
    pieces, total = strips(block)
    return pl.pallas_call(
        lambda *refs: first_kernel(*refs, pieces=pieces, half=total // 2, last=last),
        out_shape=(square(block),) * 2,
        in_specs=[SMEM, VMEM, VMEM],
        out_specs=(VMEM,) * 2,
        scratch_shapes=[pltpu.VMEM((total, LANES), jnp.float32)] + small(3),
        compiler_params=limit(12),
        name="first",
    )(places, mine, other)


def start_second(places, mine, other, inverse_first, block, last):
    pieces, total = strips(block)
    return pl.pallas_call(
        lambda *refs: second_kernel(*refs, pieces=pieces, half=total // 2, last=last),
        out_shape=(square(block),) * 3,
        in_specs=[SMEM, VMEM, VMEM, VMEM],
        out_specs=(VMEM,) * 3,
        scratch_shapes=[pltpu.VMEM((total, LANES), jnp.float32)] + small(3),
        compiler_params=limit(12),
        name="second",
    )(places, mine, other, inverse_first)


def finish(work, out, first):
    block = work.shape[0]
    return pl.pallas_call(
        lambda *refs: rest_kernel(*refs, first=first),
        out_shape=square(block),
        in_specs=[VMEM, VMEM],
        out_specs=VMEM,
        scratch_shapes=[pltpu.VMEM((block, block), jnp.float32)] + small(3),
        compiler_params=limit(12),
        name="finish",
    )(work, out)


def stage_bits(cols, stage):
    if stage == 0:
        return 1, 1
    bits = [1 << b for b in range(1, cols.bit_length() - 1)]
    turn = len(bits) // 2
    return bits[stage - 1], (bits[turn:] + bits[:turn])[stage - 1]


def stage_pairs(cols, stage):
    first, second = stage_bits(cols, stage)
    return [(i, i ^ (second if i & 1 else first)) for i in range(cols)]


def bit_here(places, cols, stage):
    first, second = stage_bits(cols, stage)
    return first + places[PLACE_SIDE] * (second - first)


def differs(places, root, mine, bit):
    return ((places[root] ^ places[mine]) & bit) != 0


def start_here(places, cols, stages, packed):
    start, size = jnp.int32(0), packed
    for stage in range(stages):
        size //= 2
        start = start + jnp.where((places[COL] & bit_here(places, cols, stage)) != 0, size, 0)
    return start


def chosen(value, received, start, low, size, bound, flags):
    at = start + low + lax.broadcasted_iota(jnp.int32, (size, LANES), 0)
    wanted = jnp.where(at < bound, flags[0].astype(jnp.int32), flags[1].astype(jnp.int32))
    return jnp.where(wanted == 1, received[low : low + size, :], value[low : low + size, :])


def scatter_kernel(places, value, received, *outs, cols, stage, packed, bound):
    size = value.shape[0]
    start = start_here(places, cols, stage + 1, packed)
    bit = bit_here(places, cols, stage)
    flags = [differs(places, ROOT_COL + s, COL, bit) for s in range(2)]
    if len(outs) == 1:
        outs[0][...] = chosen(value, received, start, 0, size, bound, flags)
        return
    keep, send = outs
    low = chosen(value, received, start, 0, size // 2, bound, flags)
    high = chosen(value, received, start, size // 2, size // 2, bound, flags)
    upper = (places[COL] & bit_here(places, cols, stage + 1)) != 0

    @pl.when(upper)
    def _():
        keep[...] = high
        send[...] = low

    @pl.when(jnp.logical_not(upper))
    def _():
        keep[...] = low
        send[...] = high


def scatter(places, value, received, cols, stage, packed, bound, final):
    size = value.shape[0]
    shape = jax.ShapeDtypeStruct((size if final else size // 2, LANES), jnp.float32)
    return pl.pallas_call(
        lambda *refs: scatter_kernel(*refs, cols=cols, stage=stage, packed=packed, bound=bound),
        out_shape=(shape,) * (1 if final else 2),
        in_specs=[SMEM, VMEM, VMEM],
        out_specs=(VMEM,) * (1 if final else 2),
        compiler_params=limit(8),
        name="scatter",
    )(places, value, received)


def spread_kernel(places, value, received, out, *, cols, stages, bit, packed, bound):
    start = start_here(places, cols, stages, packed)
    flags = [differs(places, ROOT_ROW + s, ROW, bit) for s in range(2)]
    out[...] = chosen(value, received, start, 0, value.shape[0], bound, flags)


def spread(places, value, received, cols, stages, bit, packed, bound):
    return pl.pallas_call(
        lambda *refs: spread_kernel(*refs, cols=cols, stages=stages, bit=bit, packed=packed, bound=bound),
        out_shape=jax.ShapeDtypeStruct(value.shape, value.dtype),
        in_specs=[SMEM, VMEM, VMEM],
        out_specs=VMEM,
        compiler_params=limit(8),
        name="spread",
    )(places, value, received)


def gather_kernel(places, value, received, out, *, cols, stage):
    size = value.shape[0]
    upper = (places[COL] & bit_here(places, cols, stage)) != 0

    @pl.when(upper)
    def _():
        out[:size, :] = received[...]
        out[size:, :] = value[...]

    @pl.when(jnp.logical_not(upper))
    def _():
        out[:size, :] = value[...]
        out[size:, :] = received[...]


def gather(places, value, received, cols, stage):
    return pl.pallas_call(
        lambda *refs: gather_kernel(*refs, cols=cols, stage=stage),
        out_shape=jax.ShapeDtypeStruct((2 * value.shape[0], LANES), value.dtype),
        in_specs=[SMEM, VMEM, VMEM],
        out_specs=VMEM,
        compiler_params=limit(8),
        name="gather",
    )(places, value, received)


def copy_either(flag, source, other, target, sem):
    @pl.when(flag)
    def _():
        pltpu.make_async_copy(source, target, sem).start()

    @pl.when(jnp.logical_not(flag))
    def _():
        pltpu.make_async_copy(other, target, sem).start()


def ring_kernel(places, matrix, *rest, at):
    *arrived, out, sems = rest
    size = out.shape[1]
    for s in range(2):
        own = matrix.at[pl.ds(pl.multiple_of(places[TOP + s] + at, 8), size), :]
        if arrived:
            copy_either(places[DISTANCE + s] == 0, own, arrived[0].at[s], out.at[s], sems.at[s])
        else:
            pltpu.make_async_copy(own, out.at[s], sems.at[s]).start()
    for s in range(2):
        pltpu.make_async_copy(matrix.at[pl.ds(0, size), :], out.at[s], sems.at[s]).wait()


def ring_payload(places, matrix, block, step, arrived):
    size = block // CHUNKS
    return pl.pallas_call(
        lambda *refs: ring_kernel(*refs, at=min(step, CHUNKS - 1) * size),
        out_shape=jax.ShapeDtypeStruct((2, size, matrix.shape[1]), matrix.dtype),
        in_specs=[SMEM, ANY] + [ANY] * len(arrived[-1:]),
        out_specs=HBM,
        scratch_shapes=[pltpu.SemaphoreType.DMA((2,))],
        compiler_params=limit(4),
        name="payload",
    )(places, matrix, *arrived[-1:])


def half_kernel(places, matrix, *rest, which):
    *received, out, sem = rest
    half, block = out.shape
    side = places[PLACE_SIDE]
    if not received:
        side = 1 - side
    row = pl.multiple_of(side * half, 8)
    lane = pl.multiple_of(places[EDGE + which], LANES)
    own = matrix.at[pl.ds(row, half), pl.ds(lane, block)]
    if received:
        copy_either(differs(places, ROOT_COL + which, COL, 1), received[0], own, out, sem.at[0])
    else:
        pltpu.make_async_copy(own, out, sem.at[0]).start()
    pltpu.make_async_copy(matrix.at[pl.ds(0, half), pl.ds(0, block)], out, sem.at[0]).wait()


def panel_half(places, matrix, block, which, *received):
    return pl.pallas_call(
        lambda *refs: half_kernel(*refs, which=which),
        out_shape=jax.ShapeDtypeStruct((matrix.shape[0] // 2, block), matrix.dtype),
        in_specs=[SMEM, ANY] + [ANY] * len(received),
        out_specs=HBM,
        scratch_shapes=[pltpu.SemaphoreType.DMA((1,))],
        compiler_params=limit(4),
        name="half",
    )(places, matrix, *received)


def pick_kernel(places, value, received, out, sem, *, cols, stage, which):
    flag = differs(places, ROOT_COL + which, COL, bit_here(places, cols, stage))
    copy_either(flag, received, value, out, sem.at[0])
    pltpu.make_async_copy(value, out, sem.at[0]).wait()


def pick(places, value, received, cols, stage, which):
    return pl.pallas_call(
        lambda *refs: pick_kernel(*refs, cols=cols, stage=stage, which=which),
        out_shape=jax.ShapeDtypeStruct(value.shape, value.dtype),
        in_specs=[SMEM, ANY, ANY],
        out_specs=HBM,
        scratch_shapes=[pltpu.SemaphoreType.DMA((1,))],
        compiler_params=limit(4),
        name="pick",
    )(places, value, received)


def split(value):
    high = value.astype(jnp.bfloat16)
    return high, (value - high.astype(jnp.float32)).astype(jnp.bfloat16)


def three(left, right):
    def one(a, b):
        return lax.dot_general(a, b, (((1,), (0,)), ((), ())), preferred_element_type=jnp.float32)

    return one(left[0], right[0]) + (one(left[0], right[1]) + one(left[1], right[0]))


def rows_kernel(
    places, pattern, row_order, inverse0, lower, inverse1, *rest, block, tall
):
    own0, other0, own1, other1, full, left_high, left_low, panel, scaled, high_out, low_out, sems, out_sems = rest
    exact = lax.Precision.HIGHEST
    half = tall * block // 2
    side = places[PLACE_SIDE]
    for s, (own, other) in enumerate(((own0, other0), (own1, other1))):
        for n, (source, which) in enumerate(((own, side), (other, 1 - side))):
            at = pl.multiple_of(which * half, 8)
            pltpu.make_async_copy(source, panel.at[s, pl.ds(at, half), :], sems.at[s, n]).start()
    zeros = jnp.zeros((block, block), jnp.bfloat16)
    ids = [row_order[places[ROW] * tall + t] for t in range(tall)]
    for s in range(2):
        for n, source in enumerate((own0, other0)):
            pltpu.make_async_copy(source, panel.at[s, pl.ds(0, half), :], sems.at[s, n]).wait()

        def step(t, carry):
            name = row_order[places[ROW] * tall + t]
            linked = pattern[name, s] == 1
            rows = pl.ds(pl.multiple_of(t * block, block), block)
            lanes = slice(s * block, (s + 1) * block)

            @pl.when(linked)
            def _():
                if s == 0:
                    value = dot_nt(panel[0, rows, :], inverse0[...], exact)
                else:
                    value = panel[1, rows, :] - dot_nt(scaled[0, rows, :], lower[...], exact)
                    value = dot_nt(value, inverse1[...], exact)
                scaled[s, rows, :] = value
                high, low = split(value)
                high_out[rows, lanes] = high
                low_out[rows, lanes] = low

            @pl.when(jnp.logical_not(linked & (name > s)))
            def _():
                high_out[rows, lanes] = zeros
                low_out[rows, lanes] = zeros

            @pl.when(jnp.logical_not(linked))
            def _():
                scaled[s, rows, :] = jnp.zeros((block, block), jnp.float32)

            return carry

        lax.fori_loop(0, tall, step, 0)
        pltpu.make_async_copy(scaled.at[s], full.at[s], out_sems.at[s]).start()
    copies = [pltpu.make_async_copy(high_out, left_high, out_sems.at[2])]
    copies.append(pltpu.make_async_copy(low_out, left_low, out_sems.at[3]))
    for copy in copies:
        copy.start()
    for s in range(2):
        pltpu.make_async_copy(scaled.at[s], full.at[s], out_sems.at[s]).wait()
    for copy in copies:
        copy.wait()


def scale_rows(places, pattern, row_order, inverse0, lower, inverse1, halves, block, tall):
    dma = pltpu.SemaphoreType.DMA
    high = ((tall * block, 2 * block), jnp.bfloat16)
    both = ((2, tall * block, block), jnp.float32)
    return pl.pallas_call(
        lambda *refs: rows_kernel(*refs, block=block, tall=tall),
        out_shape=tuple(jax.ShapeDtypeStruct(*kind) for kind in (both, high, high)),
        in_specs=[SMEM] * 3 + [VMEM] * 3 + [ANY] * 4,
        out_specs=(HBM,) * 3,
        scratch_shapes=[pltpu.VMEM(*kind) for kind in (both, both, high, high)] + [dma((2, 2)), dma((4,))],
        compiler_params=limit(36),
        name="rows",
    )(places, pattern, row_order, inverse0, lower, inverse1, *halves)


def tail_kernel(
    places, pattern, row_order, col_order, inverse0, lower, inverse1, full, high_in, low_in, matrix, *rest,
    block, tall, broad, chunks
):
    arrived = rest[:-11]
    out, current, slab, center, left_high, left_low, right_high, right_low, in_sems, slab_sems, out_sems = rest[-11:]
    exact = lax.Precision.HIGHEST
    size = block // chunks
    for s in range(2):
        distance = places[DISTANCE + s]
        for k in range(chunks):
            target = slab.at[s, pl.ds(k * size, size), :]

            @pl.when(distance == 0)
            def _():
                source = matrix.at[pl.ds(pl.multiple_of(places[TOP + s] + k * size, 8), size), :]
                pltpu.make_async_copy(source, target, slab_sems.at[s, k]).start()

            for d in range(1, len(arrived) - chunks + 2):

                @pl.when(distance == d)
                def _():
                    pltpu.make_async_copy(arrived[k + d - 1].at[s], target, slab_sems.at[s, k]).start()

    pltpu.make_async_copy(high_in, left_high, in_sems.at[tall]).start()
    pltpu.make_async_copy(low_in, left_low, in_sems.at[tall + 1]).start()
    for t in range(tall):
        rows = pl.ds(t * block, block)
        pltpu.make_async_copy(matrix.at[rows, :], current.at[rows, :], in_sems.at[t]).start()
    for s in range(2):
        for k in range(chunks):
            target = slab.at[s, pl.ds(k * size, size), :]
            pltpu.make_async_copy(matrix.at[pl.ds(0, size), :], target, slab_sems.at[s, k]).wait()
    zeros = jnp.zeros((block, block), jnp.bfloat16)
    for u in range(broad):
        name = col_order[places[COL] * broad + u]
        lanes = slice(u * block, (u + 1) * block)
        for s in range(2):
            rows = slice(s * block, (s + 1) * block)
            used = (pattern[name, s] == 1) & (name > s)

            @pl.when(used)
            def _():
                if s == 0:
                    value = dot_nn(inverse0[...], slab[0, :, lanes], exact)
                    slab[0, :, lanes] = value
                else:
                    value = slab[1, :, lanes] - dot_nn(lower[...], slab[0, :, lanes], exact)
                    value = dot_nn(inverse1[...], value, exact)
                high, low = split(value)
                right_high[rows, lanes] = high
                right_low[rows, lanes] = low

            @pl.when(jnp.logical_not(used))
            def _():
                right_high[rows, lanes] = zeros
                right_low[rows, lanes] = zeros
                if s == 0:
                    slab[0, :, lanes] = jnp.zeros((block, block), jnp.float32)

    triangle = lax.broadcasted_iota(jnp.int32, (block, block), 0) >= lax.broadcasted_iota(jnp.int32, (block, block), 1)
    pltpu.make_async_copy(high_in, left_high, in_sems.at[tall]).wait()
    pltpu.make_async_copy(low_in, left_low, in_sems.at[tall + 1]).wait()

    def step(t, carry):
        name = row_order[places[ROW] * tall + t]
        rows = pl.ds(pl.multiple_of(t * block, block), block)
        pltpu.make_async_copy(matrix.at[rows, :], current.at[rows, :], in_sems.at[t]).wait()
        for u in range(broad):
            column = col_order[places[COL] * broad + u]
            lanes = slice(u * block, (u + 1) * block)
            retained = (pattern[name, column] == 1) & (name >= column)

            @pl.when(retained & (column >= 2))
            def _():
                left = left_high[rows, :], left_low[rows, :]
                right = right_high[:, lanes], right_low[:, lanes]
                current[rows, lanes] = current[rows, lanes] - three(left, right)

            @pl.when(retained & (column < 2))
            def _():
                copy = pltpu.make_async_copy(full.at[column, rows, :], center, in_sems.at[tall + 2])
                copy.start()
                copy.wait()
                current[rows, lanes] = jnp.where(triangle | (name != column), center[...], 0.0)

            @pl.when(jnp.logical_not(retained))
            def _():
                current[rows, lanes] = jnp.zeros((block, block), jnp.float32)

        pltpu.make_async_copy(current.at[rows, :], out.at[rows, :], out_sems.at[t]).start()
        return carry

    lax.fori_loop(0, tall, step, 0)
    for t in range(tall):
        rows = pl.ds(t * block, block)
        pltpu.make_async_copy(current.at[rows, :], out.at[rows, :], out_sems.at[t]).wait()


def tail(places, pattern, row_order, col_order, inverse0, lower, inverse1, scaled, matrix, arrived, block):
    local_rows, width = matrix.shape
    tall, broad = local_rows // block, width // block
    dma = pltpu.SemaphoreType.DMA
    return pl.pallas_call(
        lambda *refs: tail_kernel(*refs, block=block, tall=tall, broad=broad, chunks=CHUNKS),
        out_shape=jax.ShapeDtypeStruct(matrix.shape, matrix.dtype),
        in_specs=[SMEM] * 4 + [VMEM] * 3 + [ANY] * (4 + len(arrived)),
        out_specs=HBM,
        scratch_shapes=[
            pltpu.VMEM((local_rows, width), jnp.float32),
            pltpu.VMEM((2, block, width), jnp.float32),
            pltpu.VMEM((block, block), jnp.float32),
            pltpu.VMEM((local_rows, 2 * block), jnp.bfloat16),
            pltpu.VMEM((local_rows, 2 * block), jnp.bfloat16),
            pltpu.VMEM((2 * block, width), jnp.bfloat16),
            pltpu.VMEM((2 * block, width), jnp.bfloat16),
            dma((tall + 3,)),
            dma((2, CHUNKS)),
            dma((tall,)),
        ],
        compiler_params=limit(36),
        name="tail",
    )(places, pattern, row_order, col_order, inverse0, lower, inverse1, *scaled, matrix, *arrived)


ROOT_ROW, ROOT_COL, TOP, EDGE, DISTANCE, ROW, COL, PLACE_SIDE = 0, 2, 4, 6, 8, 10, 11, 12


def barrier(*values):
    return lax.optimization_barrier(values)


def exchange(value, axis, pairs):
    return lax.ppermute(value, axis, pairs)


class Ring:
    def __init__(self, places, matrix, block, rows):
        self.places, self.matrix, self.block = places, matrix, block
        self.pairs = [(i, (i + 1) % rows) for i in range(rows)]
        self.steps = CHUNKS + rows - 2
        self.arrived = []

    def payload(self):
        if len(self.arrived) == self.steps:
            return ()
        return (ring_payload(self.places, self.matrix, self.block, len(self.arrived), self.arrived),)

    def send(self, payload):
        for value in payload:
            self.arrived.append(exchange(value, "row", self.pairs))


class Panel:
    def __init__(self, places, matrix, block, which, cols):
        self.places, self.matrix, self.block, self.which, self.cols = places, matrix, block, which, cols
        self.sent = panel_half(places, matrix, block, which)
        self.stage = 0

    def send(self):
        self.received = exchange(self.sent, "col", stage_pairs(self.cols, self.stage))

    def receive(self):
        if self.stage == 0:
            self.sent = panel_half(self.places, self.matrix, self.block, self.which, self.received)
        else:
            self.sent = pick(self.places, self.sent, self.received, self.cols, self.stage, self.which)
        self.stage += 1


def make_body(rows, cols):
    stages = cols.bit_length() - 1

    def body(matrix, pattern, row_order, col_order):
        local_rows, width = matrix.shape
        block = local_rows * rows // row_order.shape[0]
        tall = local_rows // block
        packed = strips(block)[1]
        tiles = block // LANES
        corner = tiles * (tiles + 1) // 2 * LANES
        bounds = corner, corner + tiles * tiles * LANES
        places, keep, send = pack(row_order, col_order, matrix, block, rows)
        core = stage_pairs(cols, 0)

        received = exchange(send, "col", core)
        ring = Ring(places, matrix, block, rows)
        payload = ring.payload()
        panels = [Panel(places, matrix, block, s, cols) for s in range(2)]
        ring.send(payload)
        for stage in range(stages):
            final = stage == stages - 1
            found = scatter(places, keep, received, cols, stage, packed, bounds[1], final)
            if not final:
                keep, send = found
                received = exchange(send, "col", stage_pairs(cols, stage + 1))
            if stage == 0:
                for panel in panels:
                    panel.send()
        value = found[0]
        for panel in panels:
            panel.receive()
        value, panels[0].sent, panels[1].sent, ring.arrived[0] = barrier(
            value, panels[0].sent, panels[1].sent, ring.arrived[0]
        )
        for b in range(rows.bit_length() - 1):
            received = exchange(value, "row", [(i, i ^ (1 << b)) for i in range(rows)])
            if b == 0:
                panels[0].send()
            value = spread(places, value, received, cols, stages, 1 << b, packed, bounds[0])
        value, *payload = barrier(value, *ring.payload())
        ring.send(payload)
        for stage in range(stages - 1, 0, -1):
            received = exchange(value, "col", stage_pairs(cols, stage))
            value = gather(places, value, received, cols, stage)
        mine = value
        other = exchange(mine, "col", core)
        panels[0].receive()
        mine, other, panels[0].sent = barrier(mine, other, panels[0].sent)
        panels[0].send()
        work, out = start_first(places, mine, other, block, 1)
        work, out, *payload = barrier(work, out, *ring.payload())
        ring.send(payload)
        panels[1].send()
        inverse0 = finish(work, out, 1)
        panels[0].receive()
        panels[1].receive()
        inverse0, panels[0].sent, panels[1].sent, *payload = barrier(
            inverse0, panels[0].sent, panels[1].sent, *ring.payload()
        )
        ring.send(payload)
        panels[1].send()
        lower, work, out = start_second(places, mine, other, inverse0, block, tiles - 1)
        panels[1].receive()
        for panel in panels:
            while panel.stage < stages:
                panel.send()
                panel.receive()
        work, out, panels[0].sent, panels[1].sent, *payload = barrier(
            work, out, panels[0].sent, panels[1].sent, *ring.payload()
        )
        ring.send(payload)
        others = [exchange(panel.sent, "col", core) for panel in panels]
        inverse1 = finish(work, out, tiles - 1)
        while len(ring.arrived) < ring.steps:
            ring.send(ring.payload())
        halves = panels[0].sent, others[0], panels[1].sent, others[1]
        scaled = scale_rows(places, pattern, row_order, inverse0, lower, inverse1, halves, block, tall)
        return tail(
            places, pattern, row_order, col_order, inverse0, lower, inverse1, scaled, matrix, ring.arrived, block
        )

    return body


def solution(mesh):
    in_specs = (P("row", "col"), P(), P(), P())
    out_specs = P("row", "col")
    body = make_body(mesh.shape["row"], mesh.shape["col"])
    return jax.shard_map(body, mesh=mesh, in_specs=in_specs, out_specs=out_specs, check_vma=False)
```
